128 devices in a mesh: dp: 16 (over x, z), seq: 8 (over y, core).
Axes of the slice: x: 4, y: 4, z: 4, core: 2. Of those that a mesh axis runs over, the one named last changes fastest.
Arguments:
- query_rows: bfloat16 [16384, 4096], P(('dp', 'seq')), may hold values from -60 to 60
- key_rows: bfloat16 [16384, 4096], P(('dp', 'seq')), may hold values from -5 to 5
- value_rows: bfloat16 [16384, 4096], P(('dp', 'seq')), may hold values from -12 to 12
- seg_ids: int32 [16384], P(('dp', 'seq')), may hold values from 0 to 31, as said below
- timesteps: int32 [32], replicated, may hold values from 0 to 999
- w_mod: bfloat16 [256, 4096], replicated, may hold values from -0.375 to 0.375
Outputs:
- mixed_rows: bfloat16 [16384, 4096], P(('dp', 'seq'))
The draws below stay inside these ranges and needn't reach their ends.
Inputs may be any that keep to these rules, and one draw needn't show every extreme that they name: A row's bin is seg_ids // 2, a number below the size of dp. The 128 rows of one device hold at most 16 rows of any one bin, and for every index of seq some bin holds exactly 16 rows on each device of that index. Rows of one sample lie on many devices.
All inputs are finite; a program needn't handle non-finite values.
Results may differ from the reference program's by a relative error of at most 0.0058.
Values may be sent and summed in bfloat16 or wider, within the bound.
No kernel may reach another device: no remote copies, remote signals or barrier semaphores. Data moves between devices by JAX's collectives and lax.ppermute only.
A program may use at most 128 MiB of HBM per device.

```python
import math
import jax
import jax.numpy as jnp
from jax import lax

HEADS = 32
HEAD_DIM = 128
D = 4096
FREQ = 256
TOK_DEV = 128
SEG_BIN = 2
BIN_SLOTS = 2048
ROWS = 16384
SAMPLES = 32
N_DP = 16
N_SEQ = 8


def seg_layout(key):
    devices = N_DP * N_SEQ
    mean_rows = TOK_DEV // N_DP
    key_base = jax.random.fold_in(key, 11)
    full_bins = jax.random.randint(jax.random.fold_in(key_base, 1), (N_SEQ,), 0, N_DP)

    def one_device(device):
        dev_key = jax.random.fold_in(key_base, 100 + device)
        sub_keys = jax.random.split(dev_key, 4)
        full_bin = full_bins[device % N_SEQ]
        bin_scores = jax.random.randint(sub_keys[0], (N_DP,), 0, 1 << 16) * N_DP + jnp.arange(N_DP)
        bin_scores = jnp.where(jnp.arange(N_DP) == full_bin, -1, bin_scores)
        bin_order = jnp.argsort(bin_scores)
        shifts = jax.random.randint(sub_keys[1], (N_DP // 2,), 0, mean_rows + 1)
        shifts = shifts.at[0].set(mean_rows)
        count_sorted = jnp.stack([mean_rows + shifts, mean_rows - shifts], axis=1).reshape(-1)
        bounds = jnp.cumsum(count_sorted)
        positions = jnp.arange(TOK_DEV)
        bin_slot = jnp.sum((positions[:, None] >= bounds[None, :]).astype(jnp.int32), axis=1)
        row_bins = bin_order[bin_slot]
        groups = jax.random.randint(sub_keys[2], (TOK_DEV,), 0, SEG_BIN)
        groups = groups.at[1].set(groups[0])
        sample_ids = row_bins * SEG_BIN + groups
        shuffle_scores = jax.random.randint(sub_keys[3], (TOK_DEV,), 0, 1 << 16) * TOK_DEV + positions
        shuffle = jnp.argsort(shuffle_scores)
        inverse = jnp.argsort(shuffle)
        return (sample_ids[shuffle], inverse[0], inverse[1])
    return jax.vmap(one_device)(jnp.arange(devices))


def draw_seg_ids(key, part):
    sample_ids, first_row, second_row = seg_layout(key)
    return sample_ids.reshape(-1).astype(jnp.int32)


def draw_key_rows(key, part):
    devices = N_DP * N_SEQ
    row_data = jnp.clip(jax.random.normal(jax.random.fold_in(key, 29), (devices, TOK_DEV, D), jnp.float32), -4.5, 4.5)
    return row_data.reshape(devices * TOK_DEV, D).astype(jnp.bfloat16)


def draw_query_rows(key, part):
    devices = N_DP * N_SEQ
    key_base = jax.random.fold_in(key, 31)
    row_data = jnp.clip(jax.random.normal(key_base, (devices, TOK_DEV, D), jnp.float32), -4.5, 4.5)
    return row_data.reshape(devices * TOK_DEV, D).astype(jnp.bfloat16)


def plant(drawn, key, least, top_value):
    dims = drawn.shape
    index_at = [jax.random.randint(jax.random.fold_in(key, axis), (), 0, dims[axis]) for axis in range(len(dims))]
    drawn = drawn.at[tuple(index_at)].set(least)
    longest = dims.index(max(dims))
    index_at[longest] = (index_at[longest] + 1) % dims[longest]
    return drawn.at[tuple(index_at)].set(top_value)


def shard_levels(own_key, dims, cuts, smallest, top_value):
    def one(dim, blocks):
        steps = jax.random.uniform(jax.random.fold_in(jax.random.fold_in(own_key, 6), dim), (blocks,), jnp.float32, smallest / len(cuts), top_value / len(cuts))
        return jnp.repeat(jnp.exp(steps), dims[dim] // blocks).reshape((-1,) + (1,) * (len(dims) - dim - 1))

    loudness = one(*cuts[0])
    for cut in cuts[1:]:
        loudness = loudness * one(*cut)
    return loudness


def scatter_about(rng, extent, deviation, limit, pieces=(), kind=jnp.bfloat16):
    factor_of = shard_levels(rng, extent, pieces, -0.22, 0.18) if pieces else 1.0
    values = jax.random.normal(rng, extent, jnp.float32) * deviation * factor_of
    return jnp.minimum(jnp.maximum(values, -limit), limit).astype(kind)


def setup_inputs(seed: int = 0) -> dict:
    arg_keys = jax.random.split(jax.random.key(seed), 7)
    query_rows = draw_query_rows(jax.random.fold_in(arg_keys[6], 71), 0)
    key_rows = draw_key_rows(jax.random.fold_in(arg_keys[6], 71), 0)
    value_rows = scatter_about(arg_keys[2], (ROWS, D), 2.0, 12.0, ((0, 128),))
    seg_ids = draw_seg_ids(jax.random.fold_in(arg_keys[6], 71), 0)
    timesteps = plant(jax.random.randint(arg_keys[4], (SAMPLES,), 0, 1000), jax.random.fold_in(arg_keys[4], 1), 0, 999).astype(jnp.int32)
    w_mod = scatter_about(arg_keys[5], (FREQ, D), FREQ ** -0.5, 0.375)
    return dict(query_rows=query_rows, key_rows=key_rows, value_rows=value_rows, seg_ids=seg_ids, timesteps=timesteps, w_mod=w_mod)


def scale_rows_table(timesteps, w_mod):
    half_freq = FREQ // 2
    frequencies = jnp.exp(-math.log(10000.0) * jnp.arange(half_freq, dtype=jnp.float32) / half_freq)
    angles = timesteps.astype(jnp.float32)[:, None] * frequencies[None, :]
    embedding = jnp.concatenate([jnp.cos(angles), jnp.sin(angles)], axis=1)
    activated = jax.nn.silu(embedding).astype(jnp.bfloat16)
    return jnp.dot(activated, w_mod, preferred_element_type=jnp.float32)

def attend_bin(query_part, key_part, value_part, sample_ids):
    score_scale = 1.0 / math.sqrt(HEAD_DIM)
    same_sample = sample_ids[:, None] == sample_ids[None, :]

    def one_head(head_start):
        head_query = lax.dynamic_slice_in_dim(query_part, head_start, HEAD_DIM, 1)
        head_key = lax.dynamic_slice_in_dim(key_part, head_start, HEAD_DIM, 1)
        head_value = lax.dynamic_slice_in_dim(value_part, head_start, HEAD_DIM, 1)
        scores = jnp.dot(head_query, head_key.T, preferred_element_type=jnp.float32) * score_scale
        scores = jnp.where(same_sample, scores, -1e+30)
        row_max = lax.optimization_barrier(jnp.max(scores, axis=1, keepdims=True))
        weights = jnp.exp(scores - row_max)
        soft_probs = (weights / lax.optimization_barrier(jnp.sum(weights, axis=1, keepdims=True))).astype(jnp.bfloat16)
        return jnp.dot(soft_probs, head_value, preferred_element_type=jnp.float32).astype(jnp.bfloat16)
    head_starts = jnp.arange(HEADS, dtype=jnp.int32) * HEAD_DIM
    per_head = lax.map(one_head, head_starts)
    return jnp.transpose(per_head, (1, 0, 2)).reshape(sample_ids.shape[0], D)

def reference(query_rows, key_rows, value_rows, seg_ids, timesteps, w_mod):
    row_total = query_rows.shape[0]
    row_bins = (seg_ids // SEG_BIN).astype(jnp.int32)
    row_order = jnp.argsort(row_bins, stable=True).astype(jnp.int32)
    counts = lax.optimization_barrier(jnp.sum((row_bins[None, :] == jnp.arange(N_DP, dtype=jnp.int32)[:, None]).astype(jnp.int32), axis=1))
    starts = (jnp.cumsum(counts) - counts).astype(jnp.int32)
    order_padded = jnp.concatenate([row_order, jnp.full((BIN_SLOTS,), row_total, jnp.int32)])
    zero_row = jnp.zeros((1, D), jnp.bfloat16)
    query_padded = jnp.concatenate([query_rows, zero_row])
    key_padded = jnp.concatenate([key_rows, zero_row])
    value_padded = jnp.concatenate([value_rows, zero_row])
    ids_padded = jnp.concatenate([seg_ids, jnp.full((1,), -1, jnp.int32)])

    def one_bin(bin_number):
        picked = lax.dynamic_slice_in_dim(order_padded, starts[bin_number], BIN_SLOTS)
        live_slots = jnp.arange(BIN_SLOTS) < counts[bin_number]
        picked = jnp.where(live_slots, picked, row_total).astype(jnp.int32)
        attended = attend_bin(query_padded[picked], key_padded[picked], value_padded[picked], ids_padded[picked])
        return (picked, attended)
    picked_all, attended_all = lax.map(one_bin, jnp.arange(N_DP, dtype=jnp.int32))
    attended = jnp.zeros((row_total + 1, D), jnp.bfloat16)
    attended = attended.at[picked_all.reshape(-1)].set(attended_all.reshape(-1, D))[:row_total]
    scale_table = scale_rows_table(timesteps, w_mod)
    row_scales = scale_table[seg_ids]
    return (attended.astype(jnp.float32) * (1.0 + row_scales)).astype(jnp.bfloat16)
```

```python
import math

import jax
import jax.numpy as jnp
from jax import lax
from jax.experimental import pallas as pl
from jax.experimental.pallas import tpu as pltpu
from jax.sharding import PartitionSpec as P

HEADS = 32
HEAD_DIM = 128
FREQ = 256
SEG_BIN = 2
BINS = 16
SLOTS = 16
ROWS = 128
GROUP = 32
SIDE = 4
CORES = 2
MASKED = 131072.0
AXES = ("dp", "seq")
HALVES = ((1, 2), (0, 3))


def linear(x, y, z, core):
    return (x * SIDE + z) * (SIDE * CORES) + y * CORES + core


def head_groups():
    return [
        [linear(x, y, z, core) for x in range(SIDE) for z in half for y in range(SIDE)]
        for half in HALVES
        for core in range(CORES)
    ]


def exchange(blocks):
    return lax.all_to_all(
        blocks, AXES, 0, 0, tiled=True, axis_index_groups=head_groups()
    )


def every_device():
    return [
        (x, y, z, core)
        for x in range(SIDE)
        for y in range(SIDE)
        for z in range(SIDE)
        for core in range(CORES)
    ]


def from_chip(value):
    return lax.ppermute(
        value, AXES, [(linear(x, y, z, c), linear(x, y, z ^ 1, c)) for x, y, z, c in every_device()]
    )


def from_core(value):
    return lax.ppermute(
        value, AXES, [(linear(x, y, z, c), linear(x, y, z, c ^ 1)) for x, y, z, c in every_device()]
    )


def scale_rows_table(timesteps, w_mod):
    half_freq = FREQ // 2
    frequencies = jnp.exp(-math.log(10000.0) * jnp.arange(half_freq, dtype=jnp.float32) / half_freq)
    angles = timesteps.astype(jnp.float32)[:, None] * frequencies[None, :]
    embedding = jnp.concatenate([jnp.cos(angles), jnp.sin(angles)], axis=1)
    activated = jax.nn.silu(embedding).astype(jnp.bfloat16)
    return jnp.dot(activated, w_mod, preferred_element_type=jnp.float32)


EXTRA = 8


def split_kernel(rows_ref, *refs):
    heads_ref = refs[-1]
    for head in range(HEADS):
        heads_ref[head, 0:ROWS, :] = rows_ref[:, head * HEAD_DIM : (head + 1) * HEAD_DIM]
        if len(refs) == 2:
            heads_ref[head, ROWS : ROWS + EXTRA, :] = refs[0][...]


def split_heads(rows, extra=None):
    operands = [rows] if extra is None else [rows, extra]
    height = ROWS if extra is None else ROWS + EXTRA
    whole = pl.BlockSpec(memory_space=pltpu.VMEM)
    return pl.pallas_call(
        split_kernel,
        in_specs=[whole] * len(operands),
        out_specs=whole,
        out_shape=jax.ShapeDtypeStruct((HEADS, height, HEAD_DIM), rows.dtype),
        cost_estimate=pl.CostEstimate(flops=0, bytes_accessed=2 * 2**20, transcendentals=0),
        name="split_heads",
    )(*operands)


def one_hot(target_row):
    slot = lax.broadcasted_iota(jnp.int32, (BINS * SLOTS, ROWS), 0)
    return (slot == target_row).astype(jnp.float32).astype(jnp.bfloat16)


def id_row(ref, source):
    return ref[source, ROWS : ROWS + EXTRA, :].astype(jnp.float32)[0:1, :].astype(jnp.int32)


def target_row(ids):
    bins = ids >> 1
    hits = lax.broadcasted_iota(jnp.int32, (BINS, ROWS), 0) == bins
    before = lax.broadcasted_iota(jnp.int32, (ROWS, ROWS), 0) < lax.broadcasted_iota(
        jnp.int32, (ROWS, ROWS), 1
    )
    ranks = jnp.dot(
        hits.astype(jnp.float32).astype(jnp.bfloat16),
        before.astype(jnp.float32).astype(jnp.bfloat16),
        preferred_element_type=jnp.float32,
    )
    rank = jnp.sum(jnp.where(hits, ranks, 0.0), axis=0, keepdims=True)
    return bins * SLOTS + rank.astype(jnp.int32)


def sample_marks(ids):
    mark = lax.broadcasted_iota(jnp.int32, (HEAD_DIM, ROWS), 0)
    return (mark == (ids & 1)).astype(jnp.float32).astype(jnp.bfloat16)


SOURCES_STEP = 8


def spread_kernel(kind, id_ref, part_ref, out_ref):
    for source in range(SOURCES_STEP):
        ids = id_row(id_ref, source)
        place = one_hot(target_row(ids))
        slotted = jnp.dot(place, part_ref[source, 0:ROWS, :], preferred_element_type=jnp.float32)
        if kind != "value":
            marked = lax.dot_general(
                place, sample_marks(ids), (((1,), (1,)), ((), ())), preferred_element_type=jnp.float32
            )
            if kind == "key":
                marked = marked * MASKED - MASKED
            slotted = jnp.concatenate([slotted, marked], axis=1)
        out_ref[:, source * SLOTS : (source + 1) * SLOTS, :] = slotted.astype(jnp.bfloat16).reshape(
            BINS, SLOTS, slotted.shape[1]
        )


def spread(kind, key_part, part):
    width = HEAD_DIM if kind == "value" else 2 * HEAD_DIM
    return pl.pallas_call(
        lambda *refs: spread_kernel(kind, *refs),
        grid=(GROUP // SOURCES_STEP,),
        in_specs=[
            pl.BlockSpec((SOURCES_STEP, ROWS + EXTRA, HEAD_DIM), lambda i: (i, 0, 0)),
            pl.BlockSpec((SOURCES_STEP,) + part.shape[1:], lambda i: (i, 0, 0)),
        ],
        out_specs=pl.BlockSpec((BINS, SOURCES_STEP * SLOTS, width), lambda i: (0, i, 0)),
        out_shape=jax.ShapeDtypeStruct((BINS, GROUP * SLOTS, width), jnp.bfloat16),
        compiler_params=pltpu.CompilerParams(vmem_limit_bytes=32 * 2**20),
        cost_estimate=pl.CostEstimate(
            flops=2 * GROUP * BINS * SLOTS * ROWS * width,
            bytes_accessed=2**20 + BINS * GROUP * SLOTS * width * 2,
            transcendentals=0,
        ),
        name="spread_" + kind,
    )(key_part, part)


QUERY_TILE = 512


def attend_kernel(id_ref, query_ref, *refs):
    key_refs, value_refs = refs[:4], refs[4:8]
    out_ref, slots_ref = refs[8:]
    step = pl.program_id(0)
    score_scale = 1.0 / math.sqrt(HEAD_DIM)
    length = GROUP * SLOTS
    ones = jnp.ones((length, HEAD_DIM), jnp.bfloat16)
    for tile in range(length // QUERY_TILE):
        rows = slice(tile * QUERY_TILE, (tile + 1) * QUERY_TILE)
        query = query_ref[0, rows, :]
        scores = [
            lax.dot_general(
                query, key_ref[0], (((1,), (1,)), ((), ())), preferred_element_type=jnp.float32
            )
            for key_ref in key_refs
        ]
        row_max = jnp.max(
            jnp.maximum(jnp.maximum(scores[0], scores[1]), jnp.maximum(scores[2], scores[3])),
            axis=1,
            keepdims=True,
        )
        total = None
        for part, value_ref in zip(scores, value_refs):
            weights = jnp.exp((part - row_max) * score_scale).astype(jnp.bfloat16)
            wide = jnp.concatenate([value_ref[0], ones], axis=1)
            product = jnp.dot(weights, wide, preferred_element_type=jnp.float32)
            total = product if total is None else total + product
        slots_ref[step, rows, :] = (total[:, :HEAD_DIM] / total[:, HEAD_DIM:]).astype(jnp.bfloat16)

    @pl.when(step == BINS - 1)
    def _():
        for source in range(GROUP):
            place = one_hot(target_row(id_row(id_ref, source)))
            held = slots_ref[:, source * SLOTS : (source + 1) * SLOTS, :].reshape(
                BINS * SLOTS, HEAD_DIM
            )
            out_ref[source] = lax.dot_general(
                place, held, (((0,), (0,)), ((), ())), preferred_element_type=jnp.float32
            ).astype(jnp.bfloat16)


def attend(key_part, query, keys, values):
    length = GROUP * SLOTS
    wide = pl.BlockSpec((1, length, 2 * HEAD_DIM), lambda i: (i, 0, 0))
    narrow = pl.BlockSpec((1, length, HEAD_DIM), lambda i: (i, 0, 0))
    pairs = BINS * length * length * len(keys)
    return pl.pallas_call(
        attend_kernel,
        grid=(BINS,),
        in_specs=[pl.BlockSpec((GROUP, ROWS + EXTRA, HEAD_DIM), lambda i: (0, 0, 0)), wide]
        + [wide] * len(keys)
        + [narrow] * len(values),
        out_specs=pl.BlockSpec((GROUP, ROWS, HEAD_DIM), lambda i: (0, 0, 0)),
        out_shape=jax.ShapeDtypeStruct((GROUP, ROWS, HEAD_DIM), jnp.bfloat16),
        scratch_shapes=[pltpu.VMEM((BINS, length, HEAD_DIM), jnp.bfloat16)],
        compiler_params=pltpu.CompilerParams(vmem_limit_bytes=48 * 2**20),
        cost_estimate=pl.CostEstimate(
            flops=8 * pairs * HEAD_DIM, bytes_accessed=28 * 2**20, transcendentals=pairs
        ),
        name="attend",
    )(key_part, query, *keys, *values)


def finish_kernel(heads_ref, scale_ref, out_ref):
    for head in range(HEADS):
        columns = slice(head * HEAD_DIM, (head + 1) * HEAD_DIM)
        out_ref[:, columns] = (
            heads_ref[head].astype(jnp.float32) * (1.0 + scale_ref[:, columns])
        ).astype(jnp.bfloat16)


def finish(heads, row_scales):
    whole = pl.BlockSpec(memory_space=pltpu.VMEM)
    return pl.pallas_call(
        finish_kernel,
        in_specs=[whole, whole],
        out_specs=whole,
        out_shape=jax.ShapeDtypeStruct((ROWS, HEADS * HEAD_DIM), jnp.bfloat16),
        cost_estimate=pl.CostEstimate(flops=2**20, bytes_accessed=4 * 2**20, transcendentals=0),
        name="finish",
    )(heads, row_scales)


def shards(query_rows, key_rows, value_rows, seg_ids, timesteps, w_mod):
    def gathered(own):
        chip = from_chip(own)
        return own, chip, from_core(own), from_core(chip)

    id_rows = jnp.broadcast_to(seg_ids.astype(jnp.bfloat16)[None, :], (EXTRA, ROWS))
    key_parts = gathered(exchange(split_heads(key_rows, id_rows)))
    value_parts = gathered(exchange(split_heads(value_rows)))
    own_query = exchange(split_heads(query_rows))

    keys = [spread("key", p, p) for p in key_parts]
    values = [spread("value", k, p) for k, p in zip(key_parts, value_parts)]
    query = spread("query", key_parts[0], own_query)
    home = exchange(attend(key_parts[0], query, keys, values))

    scale_table = scale_rows_table(timesteps, w_mod)
    lookup = (
        seg_ids[:, None] == jnp.arange(scale_table.shape[0], dtype=jnp.int32)[None, :]
    ).astype(jnp.float32)
    row_scales = jnp.dot(
        lookup, scale_table, precision=lax.Precision.HIGHEST, preferred_element_type=jnp.float32
    )
    return finish(home, row_scales)


def solution(mesh):
    placed = (
        P(("dp", "seq"), None),
        P(("dp", "seq"), None),
        P(("dp", "seq"), None),
        P(("dp", "seq")),
        P(),
        P(),
    )
    return jax.shard_map(
        shards, mesh=mesh, in_specs=placed, out_specs=P(("dp", "seq"), None), check_vma=False
    )
```

```python
import math

import jax
import jax.numpy as jnp
from jax import lax
from jax.experimental import pallas as pl
from jax.experimental.pallas import tpu as pltpu
from jax.sharding import PartitionSpec as P

HEADS = 32
HEAD_DIM = 128
FREQ = 256
SEG_BIN = 2
BINS = 16
ROWS = 128
GROUP = 32
SIDE = 4
CORES = 2
MASKED = 131072.0
AXES = ("dp", "seq")
HALVES = ((1, 2), (0, 3))


def linear(x, y, z, core):
    return (x * SIDE + z) * (SIDE * CORES) + y * CORES + core


def head_groups():
    return [
        [linear(x, y, z, core) for x in range(SIDE) for z in half for y in range(SIDE)]
        for half in HALVES
        for core in range(CORES)
    ]


def exchange(blocks):
    return lax.all_to_all(
        blocks, AXES, 0, 0, tiled=True, axis_index_groups=head_groups()
    )


def every_device():
    return [
        (x, y, z, core)
        for x in range(SIDE)
        for y in range(SIDE)
        for z in range(SIDE)
        for core in range(CORES)
    ]


def from_chip(value):
    return lax.ppermute(
        value, AXES, [(linear(x, y, z, c), linear(x, y, z ^ 1, c)) for x, y, z, c in every_device()]
    )


def from_core(value):
    return lax.ppermute(
        value, AXES, [(linear(x, y, z, c), linear(x, y, z, c ^ 1)) for x, y, z, c in every_device()]
    )


def scale_rows_table(timesteps, w_mod):
    half_freq = FREQ // 2
    frequencies = jnp.exp(-math.log(10000.0) * jnp.arange(half_freq, dtype=jnp.float32) / half_freq)
    angles = timesteps.astype(jnp.float32)[:, None] * frequencies[None, :]
    embedding = jnp.concatenate([jnp.cos(angles), jnp.sin(angles)], axis=1)
    activated = jax.nn.silu(embedding).astype(jnp.bfloat16)
    return jnp.dot(activated, w_mod, preferred_element_type=jnp.float32)


EXTRA = 8


def split_kernel(rows_ref, *refs):
    heads_ref = refs[-1]
    if len(refs) == 2:
        ids = jnp.broadcast_to(refs[0][...].astype(jnp.float32), (EXTRA, ROWS)).astype(jnp.bfloat16)
    for head in range(HEADS):
        heads_ref[head, 0:ROWS, :] = rows_ref[:, head * HEAD_DIM : (head + 1) * HEAD_DIM]
        if len(refs) == 2:
            heads_ref[head, ROWS : ROWS + EXTRA, :] = ids


def split_heads(rows, extra=None):
    operands = [rows] if extra is None else [rows, extra]
    height = ROWS if extra is None else ROWS + EXTRA
    whole = pl.BlockSpec(memory_space=pltpu.VMEM)
    return pl.pallas_call(
        split_kernel,
        in_specs=[whole] * len(operands),
        out_specs=whole,
        out_shape=jax.ShapeDtypeStruct((HEADS, height, HEAD_DIM), rows.dtype),
        cost_estimate=pl.CostEstimate(flops=0, bytes_accessed=2 * 2**20, transcendentals=0),
        name="split_heads",
    )(*operands)


TILE = 16
PAIR = 2
WINDOW = 3 * TILE
PLACES = GROUP * ROWS
CHUNK = 128
LENGTH = PLACES + CHUNK
KEY_TILE = 256
SIZES = ((320, 1152), (320, 1408), (448, 1408), (528, 2304))
QUERY_LENGTH = GROUP * ROWS + SIZES[-1][0]
HELD = SIZES[-1][1] + KEY_TILE


def as_bf16(mask):
    return mask.astype(jnp.float32).astype(jnp.bfloat16)


def iota(shape, dimension):
    return lax.broadcasted_iota(jnp.int32, shape, dimension)


def plan(ids):
    bins = ids >> 1
    hits = [(bins == b).astype(jnp.float32) for b in range(BINS)]
    lane = iota((GROUP, ROWS), 1)
    counts = jnp.zeros((GROUP, ROWS), jnp.float32)
    for b in range(BINS):
        counts = jnp.where(lane == b, jnp.sum(hits[b], axis=1, keepdims=True), counts)
    counts = counts.astype(jnp.bfloat16)
    before = as_bf16(iota((ROWS, ROWS), 0) < iota((ROWS, ROWS), 1))
    source, other = iota((GROUP, GROUP), 0), iota((GROUP, GROUP), 1)
    start = jnp.sum(
        jnp.dot(counts, before, preferred_element_type=jnp.float32), axis=0, keepdims=True
    )
    off, pair_off = (
        (start + jnp.dot(as_bf16(other < limit), counts, preferred_element_type=jnp.float32)).astype(
            jnp.int32
        )
        for limit in (source, (source >> 1) * PAIR)
    )
    ranks = jnp.dot(
        jnp.concatenate(hits, axis=0).astype(jnp.bfloat16), before, preferred_element_type=jnp.float32
    )
    tile = pair_off >> 4
    inside = (off - tile * TILE).astype(jnp.float32)
    code = jnp.zeros((GROUP, ROWS), jnp.float32)
    for b in range(BINS):
        place = ranks[b * GROUP : (b + 1) * GROUP, :] + (inside[:, b : b + 1] + float(b * WINDOW))
        code = code + hits[b] * place
    return code.astype(jnp.int32), tile, start.astype(jnp.int32)


def windows(code_ref, pair):
    code = jnp.concatenate(
        [code_ref[pl.ds(pair * PAIR + i, 1), :] for i in range(PAIR)], axis=1
    )
    return as_bf16(iota((BINS * WINDOW, PAIR * ROWS), 0) == code)


def window_at(tile_ref, pair, b):
    return pl.ds(pl.multiple_of(tile_ref[pair * PAIR, b] * TILE, TILE), WINDOW)


def marks_of(id_row):
    marks = (iota((HEAD_DIM, ROWS), 0) == id_row).astype(jnp.float32)
    return jnp.transpose(marks)


def add_windows(tile_ref, code_ref, part_ref, id_ref, out_refs):
    for out_ref in out_refs:
        out_ref[...] = jnp.zeros_like(out_ref)

    def one_pair(pair, carry):
        moved = jnp.concatenate([part_ref[pair * PAIR + i, 0:ROWS, :] for i in range(PAIR)], axis=0)
        if len(out_refs) == 2:
            marks = jnp.concatenate(
                [marks_of(id_ref[pl.ds(pair * PAIR + i, 1), :]) for i in range(PAIR)], axis=0
            )
            moved = jnp.concatenate([moved, marks.astype(jnp.bfloat16)], axis=1)
        placed = jnp.dot(
            windows(code_ref, pair), moved, preferred_element_type=jnp.float32
        ).astype(jnp.bfloat16)
        for b in range(BINS):
            here = window_at(tile_ref, pair, b)
            for i, out_ref in enumerate(out_refs):
                block = placed[b * WINDOW : (b + 1) * WINDOW, i * HEAD_DIM : (i + 1) * HEAD_DIM]
                out_ref[here, :] = out_ref[here, :] + block
        return carry

    lax.fori_loop(0, GROUP // PAIR, one_pair, 0, unroll=2)


def key_kernel(part_ref, key_ref, mark_ref, id_ref, code_ref, tile_ref, start_ref, tiles, sem):
    ids = part_ref[:, ROWS : ROWS + EXTRA, :].astype(jnp.float32)[:, 0:1, :]
    ids = ids.reshape(GROUP, ROWS).astype(jnp.int32)
    code, tile, start = plan(ids)
    id_ref[...] = ids
    code_ref[...] = code
    tile_ref[...] = tile
    start_ref[...] = jnp.broadcast_to(start, start_ref.shape)
    copy = pltpu.make_async_copy(tile_ref, tiles, sem)
    copy.start()
    copy.wait()
    add_windows(tiles, code_ref, part_ref, id_ref, (key_ref, mark_ref))
    number = iota((8, HEAD_DIM), 1).astype(jnp.float32).astype(jnp.bfloat16)
    for chunk in range(GROUP):
        rows = slice(chunk * ROWS, (chunk + 1) * ROWS)
        samples = lax.dot_general(
            number, mark_ref[rows, :], (((1,), (1,)), ((), ())), preferred_element_type=jnp.float32
        )
        id_ref[chunk : chunk + 1, :] = samples[0:1, :].astype(jnp.int32)
    key_ref[PLACES : PLACES + GROUP, :] = id_ref[...].astype(jnp.float32).astype(jnp.bfloat16)
    id_ref[...] = ids
    marks = mark_ref[...].astype(jnp.float32)
    mark_ref[...] = (marks * MASKED - MASKED).astype(jnp.bfloat16)


def compact_key(part):
    table = jax.ShapeDtypeStruct((GROUP, ROWS), jnp.int32)
    rows = jax.ShapeDtypeStruct((LENGTH, HEAD_DIM), jnp.bfloat16)
    whole = pl.BlockSpec(memory_space=pltpu.VMEM)
    return pl.pallas_call(
        key_kernel,
        in_specs=[whole],
        out_specs=[whole] * 6,
        out_shape=[rows, rows, table, table, table, jax.ShapeDtypeStruct((8, ROWS), jnp.int32)],
        scratch_shapes=[pltpu.SMEM((GROUP, ROWS), jnp.int32), pltpu.SemaphoreType.DMA],
        compiler_params=pltpu.CompilerParams(vmem_limit_bytes=16 * 2**20),
        cost_estimate=pl.CostEstimate(
            flops=2 * PLACES * BINS * WINDOW * 2 * HEAD_DIM, bytes_accessed=3 * 2**20, transcendentals=0
        ),
        name="compact_key",
    )(part)


def mark_kernel(*refs):
    parts = len(refs) // 3
    for id_ref, mark_ref, start_ref in zip(refs[:parts], refs[parts::2], refs[parts + 1 :: 2]):
        ids = id_ref[...].astype(jnp.float32).astype(jnp.int32)
        bins = ids >> 1
        lane = iota((1, ROWS), 1)
        start = jnp.zeros((1, ROWS), jnp.float32)
        for b in range(1, BINS + 1):
            below = jnp.sum((bins < b).astype(jnp.float32), axis=1, keepdims=True)
            start = jnp.where(lane == b, jnp.sum(below, axis=0, keepdims=True), start)
        start_ref[...] = jnp.broadcast_to(start, start_ref.shape).astype(jnp.int32)
        for chunk in range(GROUP):
            marks = marks_of(ids[chunk : chunk + 1, :])
            mark_ref[chunk * ROWS : (chunk + 1) * ROWS, :] = (marks * MASKED - MASKED).astype(
                jnp.bfloat16
            )
        mark_ref[PLACES:, :] = jnp.full((LENGTH - PLACES, HEAD_DIM), -MASKED, jnp.bfloat16)


def remote_marks(parts):
    rows = jax.ShapeDtypeStruct((LENGTH, HEAD_DIM), jnp.bfloat16)
    start = jax.ShapeDtypeStruct((8, ROWS), jnp.int32)
    found = pl.pallas_call(
        mark_kernel,
        grid=(1,),
        in_specs=[pl.BlockSpec((GROUP, HEAD_DIM), lambda i: (PLACES // GROUP, 0))] * len(parts),
        out_specs=[
            pl.BlockSpec(shape, lambda i: (0, 0))
            for _ in parts
            for shape in ((LENGTH, HEAD_DIM), (8, ROWS))
        ],
        out_shape=[rows, start] * len(parts),
        compiler_params=pltpu.CompilerParams(vmem_limit_bytes=16 * 2**20),
        cost_estimate=pl.CostEstimate(flops=2**24, bytes_accessed=3 * 2**20, transcendentals=0),
        name="remote_marks",
    )(*parts)
    return found[::2], found[1::2]


def compact_kernel(kind, tile_ref, code_ref, id_ref, part_ref, *out_refs):
    add_windows(tile_ref, code_ref, part_ref, id_ref, out_refs)


def compact(kind, tables, part):
    ids, code, tile = tables
    length = QUERY_LENGTH if kind == "query" else LENGTH
    outs = 2 if kind == "query" else 1
    whole = pl.BlockSpec(memory_space=pltpu.VMEM)
    return pl.pallas_call(
        lambda *refs: compact_kernel(kind, *refs),
        in_specs=[pl.BlockSpec(memory_space=pltpu.SMEM), whole, whole, whole],
        out_specs=[whole] * outs,
        out_shape=[jax.ShapeDtypeStruct((length, HEAD_DIM), jnp.bfloat16)] * outs,
        compiler_params=pltpu.CompilerParams(vmem_limit_bytes=16 * 2**20),
        cost_estimate=pl.CostEstimate(
            flops=2 * PLACES * BINS * WINDOW * 2 * HEAD_DIM,
            bytes_accessed=2**20 + length * outs * HEAD_DIM * 2,
            transcendentals=0,
        ),
        name="compact_" + kind,
    )(tile, code, ids, part)


def attend_kernel(tile_ref, *refs):
    start_refs, (code_ref, query_ref, own_ref), refs = refs[:4], refs[4:7], refs[7:]
    key_refs, mark_refs, value_refs = refs[:4], refs[4:8], refs[8:12]
    out_ref, held_key, held_value, rows_ref = refs[12:]
    score_scale = 1.0 / math.sqrt(HEAD_DIM)
    nothing = jnp.concatenate(
        [
            jnp.zeros((KEY_TILE, HEAD_DIM), jnp.bfloat16),
            jnp.full((KEY_TILE, HEAD_DIM), -MASKED, jnp.bfloat16),
        ],
        axis=1,
    )
    held_key[...] = jnp.zeros_like(held_key)
    held_value[...] = jnp.zeros_like(held_value)
    rows_ref[...] = jnp.zeros_like(rows_ref)

    def attend_block(first, start, held, query_rows, key_rows):
        def clear(i, carry):
            held_key[pl.ds(pl.multiple_of(held + i * KEY_TILE, TILE), KEY_TILE), :] = nothing
            return carry

        lax.fori_loop(0, (key_rows - held + (KEY_TILE - 1)) >> 8, clear, 0)
        here = pl.ds(first, query_rows)
        query = jnp.concatenate([query_ref[here, :], own_ref[here, :]], axis=1)
        edges = list(range(0, key_rows, KEY_TILE)) + [key_rows]
        tiles = [slice(low, high) for low, high in zip(edges[:-1], edges[1:])]
        scores = [
            lax.dot_general(
                query, held_key[tile, :], (((1,), (1,)), ((), ())), preferred_element_type=jnp.float32
            )
            for tile in tiles
        ]
        row_max = jnp.max(scores[0], axis=1, keepdims=True)
        for part in scores[1:]:
            row_max = jnp.maximum(row_max, jnp.max(part, axis=1, keepdims=True))
        total = None
        for part, tile in zip(scores, tiles):
            weights = jnp.exp((part - row_max) * score_scale).astype(jnp.bfloat16)
            value = held_value[tile, :]
            wide = jnp.concatenate([value, jnp.ones_like(value)], axis=1)
            product = jnp.dot(weights, wide, preferred_element_type=jnp.float32)
            total = product if total is None else total + product
        result = (total[:, :HEAD_DIM] / total[:, HEAD_DIM:]).astype(jnp.bfloat16)
        own = iota((query_rows, HEAD_DIM), 0) >= start - first
        rows_ref[here, :] = jnp.where(own, result, rows_ref[here, :])

    def one_bin(b, carry):
        held = jnp.int32(0)
        for start_ref, *part_refs in zip(start_refs, key_refs, mark_refs, value_refs):
            first = (start_ref[0, b] >> 4) * TILE
            past = ((start_ref[0, b + 1] + (TILE - 1)) >> 4) * TILE

            def one_chunk(i, carry, first=first, held=held, part_refs=part_refs):
                key_ref, mark_ref, value_ref = part_refs
                source = pl.ds(pl.multiple_of(first + i * CHUNK, TILE), CHUNK)
                target = pl.ds(pl.multiple_of(held + i * CHUNK, TILE), CHUNK)
                held_key[target, :HEAD_DIM] = key_ref[source, :]
                held_key[target, HEAD_DIM:] = mark_ref[source, :]
                held_value[target, :] = value_ref[source, :]
                return carry

            lax.fori_loop(0, (past - first + (CHUNK - 1)) >> 7, one_chunk, 0)
            held = held + (past - first)
        start = start_refs[0][0, b]
        first = pl.multiple_of((start >> 4) * TILE, TILE)
        rows = ((start_refs[0][0, b + 1] + (TILE - 1)) >> 4) * TILE - first
        taken = jnp.bool_(False)
        for query_rows, key_rows in SIZES:
            fits = (rows <= query_rows) & (held <= key_rows)
            if (query_rows, key_rows) == SIZES[-1]:
                fits = jnp.bool_(True)

            @pl.when(fits & jnp.logical_not(taken))
            def _(query_rows=query_rows, key_rows=key_rows):
                attend_block(first, start, held, query_rows, key_rows)

            taken = taken | fits
        return carry

    lax.fori_loop(0, BINS, one_bin, 0)

    def one_pair(pair, carry):
        found = jnp.concatenate(
            [rows_ref[window_at(tile_ref, pair, b), :] for b in range(BINS)], axis=0
        )
        out_ref[pl.ds(pair * PAIR, PAIR)] = (
            lax.dot_general(
                windows(code_ref, pair),
                found,
                (((0,), (0,)), ((), ())),
                preferred_element_type=jnp.float32,
            )
            .astype(jnp.bfloat16)
            .reshape(PAIR, ROWS, HEAD_DIM)
        )
        return carry

    lax.fori_loop(0, GROUP // PAIR, one_pair, 0, unroll=2)


def attend(tables, starts, query, keys, marks, values):
    scalars = pl.BlockSpec(memory_space=pltpu.SMEM)
    whole = pl.BlockSpec(memory_space=pltpu.VMEM)
    pairs = BINS * 320 * 1152
    return pl.pallas_call(
        attend_kernel,
        in_specs=[scalars] * 5 + [whole] * 15,
        out_specs=whole,
        out_shape=jax.ShapeDtypeStruct((GROUP, ROWS, HEAD_DIM), jnp.bfloat16),
        scratch_shapes=[
            pltpu.VMEM((HELD, 2 * HEAD_DIM), jnp.bfloat16),
            pltpu.VMEM((HELD, HEAD_DIM), jnp.bfloat16),
            pltpu.VMEM((QUERY_LENGTH, HEAD_DIM), jnp.bfloat16),
        ],
        compiler_params=pltpu.CompilerParams(vmem_limit_bytes=26 * 2**20),
        cost_estimate=pl.CostEstimate(
            flops=8 * pairs * HEAD_DIM, bytes_accessed=16 * 2**20, transcendentals=pairs
        ),
        name="attend",
    )(tables[2], *starts, tables[1], *query, *keys, *marks, *values)


def finish_kernel(heads_ref, scale_ref, out_ref):
    for head in range(HEADS):
        columns = slice(head * HEAD_DIM, (head + 1) * HEAD_DIM)
        out_ref[:, columns] = (
            heads_ref[head].astype(jnp.float32) * (1.0 + scale_ref[:, columns])
        ).astype(jnp.bfloat16)


def finish(heads, row_scales):
    whole = pl.BlockSpec(memory_space=pltpu.VMEM)
    return pl.pallas_call(
        finish_kernel,
        in_specs=[whole, whole],
        out_specs=whole,
        out_shape=jax.ShapeDtypeStruct((ROWS, HEADS * HEAD_DIM), jnp.bfloat16),
        cost_estimate=pl.CostEstimate(flops=2**20, bytes_accessed=4 * 2**20, transcendentals=0),
        name="finish",
    )(heads, row_scales)


def shards(query_rows, key_rows, value_rows, seg_ids, timesteps, w_mod):
    raw_key = exchange(split_heads(key_rows, seg_ids[None, :]))
    split_value, split_query = lax.optimization_barrier(
        (split_heads(value_rows), split_heads(query_rows))
    )
    own_key, own_mark, *tables, own_start = compact_key(raw_key)
    chip_raw = from_chip(raw_key)
    own_value = compact("value", tables, exchange(split_value))[0]
    chip_raw, own_value = lax.optimization_barrier((chip_raw, own_value))
    chip_key, chip_mark, _, _, _, chip_start = compact_key(chip_raw)
    core_keys = [from_core(own_key), from_core(chip_key)]
    core_marks, core_starts = remote_marks(core_keys)
    query = compact("query", tables, exchange(split_query))
    chip_value, query, core_marks, core_starts = lax.optimization_barrier(
        (from_chip(own_value), query, core_marks, core_starts)
    )
    home = exchange(
        attend(
            tables,
            [own_start, chip_start, *core_starts],
            query,
            [own_key, chip_key, *core_keys],
            [own_mark, chip_mark, *core_marks],
            [own_value, chip_value, from_core(own_value), from_core(chip_value)],
        )
    )

    scale_table = scale_rows_table(timesteps, w_mod)
    lookup = (
        seg_ids[:, None] == jnp.arange(scale_table.shape[0], dtype=jnp.int32)[None, :]
    ).astype(jnp.float32)
    row_scales = jnp.dot(
        lookup, scale_table, precision=lax.Precision.HIGHEST, preferred_element_type=jnp.float32
    )
    return finish(home, row_scales)


def solution(mesh):
    placed = (
        P(("dp", "seq"), None),
        P(("dp", "seq"), None),
        P(("dp", "seq"), None),
        P(("dp", "seq")),
        P(),
        P(),
    )
    return jax.shard_map(
        shards, mesh=mesh, in_specs=placed, out_specs=P(("dp", "seq"), None), check_vma=False
    )
```
